512 devices in a mesh: seq: 64 (over y, z_lo, core), tp: 8 (over z_hi, x).
Axes of the slice: x: 4, y: 8, z: 8 (z_hi: 2, z_lo: 4; z = z_hi * 4 + z_lo), core: 2. Of those that a mesh axis runs over, the one named last changes fastest.
Arguments:
- stream: bfloat16 [8192, 8192], P('seq', 'tp'), may hold values from -6 to 6
- hidden: bfloat16 [14336, 8192], P('seq'), may hold values from -6 to 6
- final_gain: bfloat16 [8192], P('tp'), may hold values from 0.099609375 to 1.8984375
- value_head: bfloat16 [8192], P('tp'), may hold values from -0.0625 to 0.0625
- rewards: float32 [8192], P('seq'), may hold values from -3 to 3
- kl_terms: float32 [8192], P('seq'), may hold values from -6 to 6
- resets: int32 [8192], P('seq'), may hold values 0 or 1
Outputs:
- values: float32 [8192], P('seq')
- returns: float32 [8192], P('seq')
- grad_head: float32 [8192], P('tp')
- grad_down: bfloat16 [14336, 8192], P('seq', 'tp')
The draws below stay inside these ranges and needn't reach their ends.
All inputs are finite; a program needn't handle non-finite values. No bound on the sum of `resets` on one device may be relied on, other than what follows from the above.
Results may differ from the reference program's by a relative error of at most 0.0049.
Values may be sent and summed in bfloat16 or wider, within the bound.
A program may use at most 64 MiB of HBM per device.

```python
import jax
import jax.numpy as jnp
from jax import lax

D = 8192
FF = 14336
TOKENS = 8192


def with_ends(entries, key, smallest, high):
    extent = entries.shape
    index_at = [jax.random.randint(jax.random.fold_in(key, axis), (), 0, extent[axis]) for axis in range(len(extent))]
    entries = entries.at[tuple(index_at)].set(smallest)
    longest = extent.index(max(extent))
    index_at[longest] = (index_at[longest] + 1) % extent[longest]
    return entries.at[tuple(index_at)].set(high)


def block_levels(key, dims, cuts, smallest, top_value):
    def one(dim, parts):
        heights = jax.random.uniform(jax.random.fold_in(jax.random.fold_in(key, 6), dim), (parts,), jnp.float32, smallest / len(cuts), top_value / len(cuts))
        return jnp.repeat(jnp.exp(heights), dims[dim] // parts).reshape((-1,) + (1,) * (len(dims) - dim - 1))

    factor_of = one(*cuts[0])
    for cut in cuts[1:]:
        factor_of = factor_of * one(*cut)
    return factor_of


def bell_draw(stream_key, shape, spread, most, split=(), dtype=jnp.bfloat16):
    drawn = jax.random.normal(stream_key, shape, jnp.float32) * spread
    if len(split) > 0:
        drawn = block_levels(stream_key, shape, split, -0.22, 0.18) * drawn
    return jnp.clip(drawn, min=-most, max=most).astype(dtype)


def setup_inputs(seed: int = 0) -> dict:
    arg_keys = jax.random.split(jax.random.key(seed), 8)
    return {
        "stream": bell_draw(arg_keys[0], (TOKENS, D), 1.0, 6.0, ((0, 64), (1, 8))),
        "hidden": bell_draw(arg_keys[1], (FF, TOKENS), 1.0, 6.0, ((0, 64),)),
        "final_gain": jnp.clip(1.0 + 0.18 * jax.random.normal(arg_keys[2], (D,), jnp.float32), 0.099609375, 1.8984375).astype(jnp.bfloat16),
        "value_head": bell_draw(arg_keys[3], (D,), D ** -0.5, 0.0625, ((0, 8),)),
        "rewards": bell_draw(arg_keys[4], (TOKENS,), 0.2, 3.0, ((0, 64),), jnp.float32),
        "kl_terms": bell_draw(arg_keys[5], (TOKENS,), 0.5, 6.0, ((0, 64),), jnp.float32),
        "resets": with_ends((jax.random.randint(arg_keys[6], (TOKENS,), 0, 128) < 1).astype(jnp.int32), jax.random.fold_in(arg_keys[6], 1), 0, 1),
    }


epsilon = 1e-05

def reference(stream, hidden, final_gain, value_head, rewards, kl_terms, resets):
    stream_f = stream.astype(jnp.float32)
    head_vector = final_gain.astype(jnp.float32) * value_head.astype(jnp.float32)
    inv_rms = lax.rsqrt(lax.optimization_barrier(jnp.mean(stream_f * stream_f, axis=-1)) + epsilon)
    head_dot = lax.optimization_barrier(jnp.sum(stream_f * head_vector, axis=-1))
    values = inv_rms * head_dot
    step_reward = rewards - 0.2 * kl_terms
    carry_keep = 1.0 - resets.astype(jnp.float32)

    def backward_step(carry, step_item):
        step_value = step_item[0] + step_item[1] * carry
        return (step_value, step_value)
    _, returns = lax.scan(backward_step, jnp.zeros((), jnp.float32), (step_reward, carry_keep), reverse=True)
    value_error = values - returns
    grad_head = final_gain.astype(jnp.float32) * lax.optimization_barrier(jnp.sum((value_error * inv_rms)[:, None] * stream_f, axis=0))
    width = stream.shape[1]
    dstream = (value_error[:, None] * (inv_rms[:, None] * head_vector - (inv_rms ** 3 * head_dot / width)[:, None] * stream_f)).astype(jnp.bfloat16)
    grad_down = jnp.dot(hidden, dstream, preferred_element_type=jnp.float32).astype(jnp.bfloat16)
    return (values, returns, grad_head, grad_down)
```

```python
import functools

import jax
import jax.numpy as jnp
from jax import lax
from jax.experimental import pallas as pl
from jax.experimental.pallas import tpu as pltpu
from jax.sharding import PartitionSpec as P

MESH = pl.DeviceIdType.MESH
D = 8192
EPS = 1e-05
NY, NZ, NX, NT = 8, 4, 4, 8
TOK, COLS, ROWS = 128, 1024, 224
WIDTHS = (256, 256, 256, 256)
OFFS = tuple(sum(WIDTHS[:j]) for j in range(len(WIDTHS)))
C = len(WIDTHS)
START = 3.0
HOPS = ((4, 3), (3, 4))


def ring_plan(direction):
    unit, lag = [w * 0.0055 for w in WIDTHS], 2.0
    ready, order, arrival, now, z = {}, [], {}, 0.0, 0.0
    for j in range(C):
        z += unit[j]
        ready[(0, j, 1)] = 0.0
        ready[(1, j, 1)] = 3.0 + z
    while ready:
        able = [m for m in ready if ready[m] <= now + 1e-9]
        if not able:
            now = min(ready.values())
            continue
        m = min(able, key=lambda m: (m[1], m[2], m[0]))
        del ready[m]
        plane, j, hop = m
        order.append((now, m))
        now += unit[j]
        arrival[m] = now + lag
        if hop < HOPS[direction][plane]:
            ready[(plane, j, hop + 1)] = arrival[m]
    return order, arrival


def timeline():
    todo, arrivals = [], []
    for direction in (0, 1):
        order, arrival = ring_plan(direction)
        arrivals.append(arrival)
        for t, (plane, j, hop) in order:
            if (plane, hop) != (0, 1) or t > START:
                todo.append((t, 0, 0.05, ("ring", direction, plane, j, hop)))
    todo += [(7.0, 0, 0.05, ("share", 0)), (12.0, 0, 0.05, ("share", 1))]
    todo += [(17.0, 0, 0.05, ("pass", 0)), (21.0, 0, 0.05, ("pass", 1))]
    todo += [(7.0, 1, 0.3, ("first",)), (13.0, 1, 0.4, ("second",))]
    todo += [(21.0 + 0.1 * i, 2, 0.2, ("coef", i)) for i in range(NY)]
    todo += [(27.0, 0, 0.0, ("hidden",))]
    for j in range(C):
        for d in range(-3, 5):
            if d == 4:
                t = max(arrivals[0][(0, j, 4)], arrivals[1][(1, j, 4)])
            elif d == 0:
                t = 0.0
            else:
                side = 0 if d < 0 else 1
                t = max(arrivals[side][(plane, j, abs(d))] for plane in (0, 1))
            todo.append((max(27.1, t + 0.5), 3 + j, 0.4, ("piece", j, d)))
    now, order, left = 0.0, [], dict.fromkeys(range(C), NY)
    while todo:
        able = [e for e in todo if e[0] <= now + 1e-9]
        if not able:
            now = min(e[0] for e in todo)
            continue
        e = min(able, key=lambda e: (e[1], e[0]))
        todo.remove(e)
        order.append(e[3])
        now += e[2]
        if e[3][0] == "piece":
            j = e[3][1]
            left[j] -= 1
            if left[j] == 0:
                order.append(("reduce", j))
                todo.append((now + 2.5, 1, 0.2, ("swap", j)))
        if e[3][0] == "swap":
            todo.append((now + 6.0, 1, 0.2, ("write", e[3][1])))
    return order


def kernel(*refs):
    refs = list(refs)
    take = lambda n: [refs.pop(0) for _ in range(n)]
    stream, hidden, gain, head_in, rewards, kl_terms, resets = take(7)
    values_out, returns_out, head_out, down_out = take(4)
    (X,) = take(1)
    S, ACC, P1, T2, P2 = take(C), take(C), take(C), take(C), take(C)
    H, ST, PA, PB, CO, AC, BC, GP, GQ = take(9)
    ring_send, ring_recv, swap_send, swap_recv, down_send, down_recv, small_send, small_recv, hid_send, hid_recv, local = take(11)

    s, t = lax.axis_index("seq"), lax.axis_index("tp")
    y, z, c = s // 8, (s // 2) % 4, s % 2
    zb, zp, q = z % 2, z // 2, s % 8
    h, x = t // 4, t % 4
    oz, oc = z + 1 - 2 * zb, 1 - c
    fz = z + 2 - 4 * zp
    mine = zb * 2 + c

    def seq(y, z, c):
        return (y * 4 + z) * 2 + c

    def up(d):
        return lax.rem(y + 16 + d, NY)

    def remote(src, dst, send, recv, device):
        return pltpu.make_async_remote_copy(
            src_ref=src, dst_ref=dst, send_sem=send, recv_sem=recv, device_id=device, device_id_type=MESH
        )

    def drain(ref, sem):
        pltpu.make_async_copy(ref, ref, sem).wait()

    x_copy = pltpu.make_async_copy(stream, X, local.at[0])
    x_copy.start()
    own_copies = []
    for j in range(C):
        own_copies.append(
            pltpu.make_async_copy(stream.at[:, pl.ds(OFFS[j], WIDTHS[j])], S[j].at[y, zp], local.at[1 + j])
        )
        own_copies[-1].start()

    def tokens(yy, zz, cc):
        return pl.ds(pl.multiple_of(seq(yy, zz, cc) * TOK, TOK), TOK)

    def own_hidden(yy, _):
        for p in range(2):
            pltpu.make_async_copy(hidden.at[:, tokens(yy, zb + 2 * p, c)], H.at[mine, yy, p], local.at[1 + C]).start()
        return 0

    lax.fori_loop(0, NY, own_hidden, 0)

    line = []
    for d in range(1, 8):
        other = lax.rem(q + d, 8)
        line.append((y * 8 + other, t))
    column = [(seq(up(d), z, c), t) for d in range(1, NY)]
    far = [(seq(up(d), fz, c), t) for d in range(NY)]
    rank = [(s, lax.rem(t + d, NT)) for d in range(1, NT)]
    barrier = pltpu.get_barrier_semaphore()
    peers = line + column + far[1:] + rank
    for peer in peers:
        pl.semaphore_signal(barrier, inc=1, device_id=peer, device_id_type=MESH)

    row_id = lax.broadcasted_iota(jnp.int32, (TOK, TOK), 0)
    col_id = lax.broadcasted_iota(jnp.int32, (TOK, TOK), 1)

    def to_col(row):
        return jnp.sum(jnp.where(row_id == col_id, row, 0.0), axis=1, keepdims=True)

    def to_row(col):
        return jnp.sum(jnp.where(row_id == col_id, col, 0.0), axis=0, keepdims=True)

    head = gain[...].astype(jnp.float32) * head_in[...].astype(jnp.float32)
    res_row = resets[...].astype(jnp.float32)
    before_col = jnp.sum(jnp.where(col_id < row_id, res_row, 0.0), axis=1, keepdims=True)
    before_row = jnp.sum(jnp.where(row_id < col_id, to_col(res_row), 0.0), axis=0, keepdims=True)
    total = jnp.sum(res_row, axis=1, keepdims=True)
    reward_col = to_col(rewards[...] - 0.2 * kl_terms[...])
    reach = (row_id >= col_id) & (before_col == before_row)
    local_row = jnp.sum(jnp.where(reach, reward_col, 0.0), axis=0, keepdims=True)
    pass_row = jnp.where(before_row == total, 1.0, 0.0)

    def put(ref, index, first, second):
        ref[index] = jnp.zeros((8, TOK), jnp.float32)
        ref[index, 0:1, :] = jnp.broadcast_to(first, (1, TOK))
        ref[index, 1:2, :] = jnp.broadcast_to(second, (1, TOK))

    put(PA, q, local_row[:, 0:1], pass_row[:, 0:1])
    x_copy.wait()
    xf = X[...].astype(jnp.float32)
    put(
        ST,
        t,
        to_row(jnp.sum(xf * xf, axis=1, keepdims=True)),
        to_row(jnp.sum(xf * head, axis=1, keepdims=True)),
    )

    pl.semaphore_wait(barrier, len(peers))

    sends = []

    def go(copy):
        copy.start()
        sends.append(copy)

    def small(kind, n, ref, index, to):
        for i, peer in enumerate(to):
            go(remote(ref.at[index], ref.at[index], small_send.at[n + i], small_recv.at[kind], peer))

    def ring(direction, plane, j, hop):
        step = 1 if direction == 0 else -1
        slot = S[j].at[up(-step * (hop - 1)), zp if plane == 0 else 1 - zp]
        src = stream.at[:, pl.ds(OFFS[j], WIDTHS[j])] if (plane, hop) == (0, 1) else slot
        i = ((direction * 2 + plane) * C + j) * 4 + hop - 1
        return remote(src, slot, ring_send.at[i], ring_recv.at[i], (seq(up(step), z, c), t))

    def swap(j):
        return remote(
            stream.at[:, pl.ds(OFFS[j], WIDTHS[j])], S[j].at[y, zp], swap_send.at[j], swap_recv.at[j], (seq(y, fz, c), t)
        )

    first_sends = [{m[1]: at for at, m in ring_plan(d)[0] if m[0] == 0 and m[2] == 1} for d in (0, 1)]
    small(0, 0, ST, t, rank)
    small(1, 7, PA, q, line)
    for j in range(C):
        for direction in (0, 1):
            if first_sends[direction][j] <= START:
                go(ring(direction, 0, j, 1))
        go(swap(j))

    def pair_hidden(i, p, cc):
        yy = 2 * x + i
        return remote(
            hidden.at[:, tokens(yy, 1 - zb + 2 * p, cc)], H.at[mine, yy, p],
            hid_send.at[1 + i], hid_recv.at[1 + i], (seq(y, oz, cc), t),
        )

    for i in range(2):
        for p in range(2):
            for cc in range(2):
                pair_hidden(i, p, cc).start()

    def core_hidden(yy, _):
        for p in range(2):
            remote(
                hidden.at[:, tokens(yy, zb + 2 * p, oc)], H.at[mine, yy, p],
                hid_send.at[0], hid_recv.at[0], (seq(y, z, oc), t),
            ).start()
        return 0

    lax.fori_loop(0, NY, core_hidden, 0)

    def pair_block(yy):
        return H.at[pl.ds(2 * (1 - zb), 2), yy]

    def x_copy_to(direction, i, hop):
        step = 1 if direction == 0 else -1
        owner = lax.rem(x + 8 - step * (hop - 1), NX)
        block = pair_block(2 * owner + i)
        n = 3 + (hop - 1) * 4 + direction * 2 + i
        return remote(block, block, hid_send.at[n], hid_recv.at[n], (s, h * 4 + lax.rem(x + 4 + step, NX)))

    state = {}
    seen = set()

    def arrived(direction, plane, j, hop):
        if (direction, plane, j, hop) not in seen:
            seen.add((direction, plane, j, hop))
            step = 1 if direction == 0 else -1
            i = ((direction * 2 + plane) * C + j) * 4 + hop - 1
            drain(S[j].at[up(-step * hop), zp if plane == 0 else 1 - zp], ring_recv.at[i])

    def other_in(j):
        if ("swap", j) not in seen:
            seen.add(("swap", j))
            drain(S[j].at[y, 1 - zp], swap_recv.at[j])

    def do_ring(direction, plane, j, hop):
        if hop == 1 and plane == 1:
            other_in(j)
        elif hop > 1:
            arrived(direction, plane, j, hop - 1)
        go(ring(direction, plane, j, hop))

    def x_arrived(direction, i, hop):
        step = 1 if direction == 0 else -1
        owner = lax.rem(x + 8 - step * hop, NX)
        drain(pair_block(2 * owner + i), hid_recv.at[3 + (hop - 1) * 4 + direction * 2 + i])

    def do_share(i):
        drain(pair_block(2 * x + i), hid_recv.at[1 + i])
        for direction in (0, 1):
            go(x_copy_to(direction, i, 1))

    def do_pass(i):
        direction = i
        x_arrived(direction, i, 1)
        go(x_copy_to(direction, i, 2))

    def do_first():
        drain(ST.at[pl.ds(0, 7)], small_recv.at[0])
        drain(PA.at[pl.ds(0, 7)], small_recv.at[1])
        squares, along = jnp.zeros((1, TOK), jnp.float32), jnp.zeros((1, TOK), jnp.float32)
        for i in range(NT):
            squares += ST[i, 0:1, :]
            along += ST[i, 1:2, :]
        value, keep = jnp.zeros((1, TOK), jnp.float32), jnp.ones((1, TOK), jnp.float32)
        for i in reversed(range(8)):
            value = PA[i, 0:1, :] + PA[i, 1:2, :] * value
            keep = PA[i, 1:2, :] * keep
        put(PB, y, value, keep)
        small(2, 14, PB, y, column)
        mean = squares * (1.0 / D) + EPS
        scale = lax.rsqrt(mean)
        scale = scale * (1.5 - 0.5 * mean * scale * scale)
        values = scale * along
        values_out[...] = values
        state.update(scale=scale, along=along, values=values)

    def do_second():
        drain(PB.at[pl.ds(0, 7)], small_recv.at[2])
        carry = jnp.zeros((1, TOK), jnp.float32)
        my_y, my_q = jnp.full((1, TOK), y, jnp.int32), jnp.full((1, TOK), q, jnp.int32)
        for i in reversed(range(NY)):
            carry = jnp.where(my_y < i, PB[i, 0:1, :] + PB[i, 1:2, :] * carry, carry)
        for i in reversed(range(8)):
            carry = jnp.where(my_q < i, PA[i, 0:1, :] + PA[i, 1:2, :] * carry, carry)
        returns = local_row + pass_row * carry
        returns_out[...] = returns
        scale, along = state["scale"], state["along"]
        error = state["values"] - returns
        put(CO, y * 2 + zp, error * scale, error * (scale * scale * scale * along * (1.0 / D)))
        small(3, 21, CO, y * 2 + zp, column + far)

    def do_coef(i):
        if i == 0:
            drain(CO.at[pl.ds(0, 15)], small_recv.at[3])
        for p in range(2):
            block = slice(p * TOK, (p + 1) * TOK)
            AC[i, block, :] = jnp.broadcast_to(to_col(CO[i * 2 + p, 0:1, :]), (TOK, TOK))
            BC[i, block, :] = jnp.broadcast_to(to_col(CO[i * 2 + p, 1:2, :]), (TOK, TOK))

    def do_hidden():
        drain(H.at[mine], local.at[1 + C])
        drain(H.at[zb * 2 + oc], hid_recv.at[0])
        x_arrived(0, 1, 1)
        x_arrived(1, 0, 1)
        for direction in (0, 1):
            x_arrived(direction, direction, 2)

    def do_piece(j, d):
        w, off = WIDTHS[j], OFFS[j]
        if d == 0:
            own_copies[j].wait()
            other_in(j)
        elif d == 4:
            arrived(0, 0, j, 4)
            arrived(1, 1, j, 4)
        else:
            for plane in range(2):
                arrived(0 if d < 0 else 1, plane, j, abs(d))
        yy = up(d)
        a, b = AC[yy], BC[yy]
        xs = S[j][yy].reshape(2 * TOK, w)
        grads = []
        for i in range(w // TOK):
            xi = xs[:, i * TOK : (i + 1) * TOK].astype(jnp.float32)
            n = off // TOK + i
            GP[yy, n : n + 1, :] = jnp.sum(a * xi, axis=0, keepdims=True)
            grads.append((a * head[:, n * TOK : (n + 1) * TOK] - b * xi).astype(jnp.bfloat16))
        rows = [jnp.concatenate([H[r, yy, 0], H[r, yy, 1]], axis=1) for r in range(4)]
        out = jnp.dot(
            jnp.concatenate(rows, axis=0), jnp.concatenate(grads, axis=1), preferred_element_type=jnp.float32
        ).reshape(4, ROWS, w)
        if ("sum", j) not in seen:
            seen.add(("sum", j))
            ACC[j][...] = out
        else:
            ACC[j][...] += out

    def core_copy(j, k):
        return remote(
            ACC[j].at[k * 2 + oc], P1[j].at[k], down_send.at[j * 3 + k], down_recv.at[j * 3 + k], (seq(y, z, oc), t)
        )

    def pair_copy(j):
        return remote(T2[j], P2[j], down_send.at[j * 3 + 2], down_recv.at[j * 3 + 2], (seq(y, oz, c), t))

    def do_reduce(j):
        for k in range(2):
            go(core_copy(j, k))

    def do_swap(j):
        for k in range(2):
            core_copy(j, k).wait_recv()
        T2[j][...] = (ACC[j][(1 - zb) * 2 + c] + P1[j][1 - zb]).astype(jnp.bfloat16)
        go(pair_copy(j))

    def do_write(j):
        pair_copy(j).wait_recv()
        out = ACC[j][mine] + P1[j][zb] + P2[j][...].astype(jnp.float32)
        down_out[:, OFFS[j] : OFFS[j] + WIDTHS[j]] = out.astype(jnp.bfloat16)

    events = {
        "ring": do_ring, "share": do_share, "pass": do_pass, "first": do_first, "second": do_second,
        "coef": do_coef, "hidden": do_hidden, "piece": do_piece, "reduce": do_reduce, "swap": do_swap,
        "write": do_write,
    }
    order = timeline()
    last = max(i for i, e in enumerate(order) if e[0] == "piece")
    for i, e in enumerate(order):
        events[e[0]](*e[1:])
        if i == last + 1:
            part = GP[0]
            for k in range(1, NY):
                part += GP[k]
            GQ[mine] = part
            small(4, 36, GQ, mine, [(seq(y, z, oc), t), (seq(y, oz, c), t), (seq(y, oz, oc), t)])
    drain(GQ.at[pl.ds(0, 3)], small_recv.at[4])
    sums = GQ[0] + GQ[1] + GQ[2] + GQ[3]
    gain_f = gain[...].astype(jnp.float32)
    for i in range(8):
        head_out[i : i + 1, :] = gain_f[:, i * TOK : (i + 1) * TOK] * sums[i : i + 1, :]

    for copy in sends:
        copy.wait_send()
    drain(H.at[mine], hid_send.at[0])
    for i in range(2):
        drain(pair_block(i), hid_send.at[1 + i])


def scratch():
    f32, bf16 = jnp.float32, jnp.bfloat16
    V, S = pltpu.VMEM, pltpu.SemaphoreType.DMA
    out = [V((TOK, COLS), bf16)]
    out += [V((NY, 2, TOK, w), bf16) for w in WIDTHS]
    out += [V((4, ROWS, w), f32) for w in WIDTHS]
    out += [V((2, ROWS, w), f32) for w in WIDTHS]
    out += [V((ROWS, w), bf16) for w in WIDTHS] * 2
    out += [V((4, NY, 2, ROWS, TOK), bf16)]
    out += [V((n, 8, TOK), f32) for n in (8, 8, 8, 16)]
    out += [V((NY, 2 * TOK, TOK), f32)] * 2
    out += [V((NY, 8, TOK), f32), V((4, 8, TOK), f32)]
    out += [S((16 * C,)), S((16 * C,)), S((C,)), S((C,)), S((3 * C,)), S((3 * C,))]
    out += [S((39,)), S((5,)), S((11,)), S((11,)), S((2 + C,))]
    return out


def body(stream, hidden, final_gain, value_head, rewards, kl_terms, resets):
    vmem, hbm = pl.BlockSpec(memory_space=pltpu.VMEM), pl.BlockSpec(memory_space=pl.ANY)
    f32 = jnp.float32
    values, returns, grad_head, grad_down = pl.pallas_call(
        kernel,
        out_shape=(
            jax.ShapeDtypeStruct((1, TOK), f32),
            jax.ShapeDtypeStruct((1, TOK), f32),
            jax.ShapeDtypeStruct((8, TOK), f32),
            jax.ShapeDtypeStruct((ROWS, COLS), jnp.bfloat16),
        ),
        in_specs=[hbm, hbm] + [vmem] * 5,
        out_specs=(vmem,) * 4,
        scratch_shapes=scratch(),
        compiler_params=pltpu.CompilerParams(
            collective_id=0, has_side_effects=True, vmem_limit_bytes=60 * 1024 * 1024
        ),
    )(
        stream,
        hidden,
        final_gain.reshape(1, COLS),
        value_head.reshape(1, COLS),
        rewards.reshape(1, TOK),
        kl_terms.reshape(1, TOK),
        resets.reshape(1, TOK),
    )
    return (values.reshape(TOK), returns.reshape(TOK), grad_head.reshape(COLS), grad_down)


def solution(mesh):
    placed = (P("seq", "tp"), P("seq", None), P("tp"), P("tp"), P("seq"), P("seq"), P("seq"))
    return jax.shard_map(
        body,
        mesh=mesh,
        in_specs=placed,
        out_specs=(P("seq"), P("seq"), P("tp"), P("seq", "tp")),
        check_vma=False,
    )
```

```python
import functools

import jax
import jax.numpy as jnp
from jax import lax
from jax.experimental import pallas as pl
from jax.experimental.pallas import tpu as pltpu
from jax.sharding import PartitionSpec as P

MESH = pl.DeviceIdType.MESH
D = 8192
EPS = 1e-05
NY, NZ, NX, NT = 8, 4, 4, 8
TOK, COLS, ROWS = 128, 1024, 224
WIDTHS = (256, 256, 256, 256)
OFFS = tuple(sum(WIDTHS[:j]) for j in range(len(WIDTHS)))
C = len(WIDTHS)
LIMIT = {1: 1}
ROUND_FIRST = tuple(LIMIT)
FAR = {j: tuple(d for d in sorted(range(-3, 5), key=abs) if abs(d) > LIMIT[j]) for j in LIMIT}
HOPS = ((4, 3), (3, 4))
GROUPS = (("A", "B", "C"), ((-1, 0, 1, 2), (-2, 3, -3, 4)))
LAST_GROUPS = (("A", "B", "C"), ((0, 1), (-1, 2), (-2, 3), (-3, 4)))
QUARTERS = {"A": (0,), "B": (-1, 1), "C": (2,)}
START = 2.0
UNIT = tuple(w * 0.0055 for w in WIDTHS)
LAG = 2.0
FIRST, SECOND, COEF = 4.5, 11.5, 21.5
LOCAL, SHARE, PASS, LAST_HIDDEN = 15.0, (6.5, 9.0, 13.0, 17.0), (11.5, 14.2, 18.0, 22.0), 27.5
PAIR, AWAY = (0.0, 0.0, 4.2, 8.0), (2.6, 6.8, 10.5, 12.0)
SWAP, OVER = (10.5, 14.5, 18.0, 21.0), 17.0


def hops(direction, plane, j):
    return min(LIMIT[j], HOPS[direction][1]) if plane == 1 and j in LIMIT else HOPS[direction][plane]


ARRIVALS = {}
for _direction in (0, 1):
    for _plane in (0, 1):
        for _j in range(C):
            for _hop in range(hops(_direction, _plane, _j)):
                ARRIVALS[_direction, _plane, _j, _hop + 1] = len(ARRIVALS)


def ring_plan(direction):
    ready, order, arrival, now, due = {}, [], {}, 0.0, 0.0
    begin = []
    for j in range(C):
        begin.append(due - (4.0 if j == C - 1 else 0.0))
        due += UNIT[j] * sum(hops(direction, plane, j) for plane in (0, 1))
        ready[(0, j, 1)] = 0.0
        ready[(1, j, 1)] = SWAP[j]
    while ready:
        able = [m for m in ready if ready[m] <= now + 1e-9]
        if not able:
            now = min(ready.values())
            continue
        m = min(able, key=lambda m: (begin[m[1]] + 1.5 * (m[2] - 1), m[2], m[0]))
        del ready[m]
        plane, j, hop = m
        order.append((now, m))
        now += UNIT[j]
        arrival[m] = now + LAG
        if hop < hops(direction, plane, j):
            ready[(plane, j, hop + 1)] = arrival[m]
    return order, arrival


def timeline():
    todo, arrivals = [], []
    for direction in (0, 1):
        order, arrival = ring_plan(direction)
        arrivals.append(arrival)
        for t, (plane, j, hop) in order:
            if (plane, hop) != (0, 1) or t > START:
                todo.append((t, 0, 0.05, ("ring", direction, plane, j, hop)))
    todo += [(PAIR[k], 0, 0.05, ("pair", k)) for k in (2, 3)]
    todo += [(AWAY[j], 0, 0.05, ("away", j)) for j in range(C)]
    todo += [(SHARE[k], 0, 0.05, ("share", k)) for k in range(4)]
    todo += [(PASS[k], 0, 0.05, ("pass", k)) for k in range(4)]
    todo += [(LOCAL, 1, 0.5, ("local",)), (FIRST, 1, 0.2, ("first",)), (SECOND, 1, 0.4, ("second",))]
    todo += [(COEF + 0.1 * i, 2, 0.2, ("coef", i)) for i in range(NY)]
    hidden = {"A": SHARE[3] + 0.5, "B": PASS[3] + 0.3, "C": LAST_HIDDEN}
    groups = [LAST_GROUPS if j == C - 1 else GROUPS for j in range(C)]
    for j in range(C):
        times, over = ({}, {}), []
        for d in sorted(range(-3, 5), key=abs):
            own = 0.0 if d == 0 else arrivals[0 if d < 0 or d == 4 else 1][(0, j, abs(d))]
            times[0][d] = own
            if d in FAR.get(j, ()):
                own = max(own, OVER + 0.7 * len(over))
                over.append(d)
                todo.append((own, 0, 0.05, ("over", j, d)))
                times[1][d] = own + 5.0
            else:
                times[1][d] = SWAP[j] if d == 0 else arrivals[0 if d < 0 else 1][(1, j, abs(d))]
        for plane in (0, 1):
            for group in groups[j][plane]:
                if plane == 0:
                    n, t = 2 * len(QUARTERS[group]), max(hidden[group], *times[0].values())
                else:
                    n, t = len(group), max(hidden["C"], *(times[1][d] for d in group))
                todo.append((max(COEF + 1.5, t + 0.5), 3 + j, 0.05 + 0.135 * n, ("piece", j, plane, group)))
    now, order, left = 0.0, [], {j: len(groups[j][0]) + len(groups[j][1]) for j in range(C)}
    while todo:
        able = [e for e in todo if e[0] <= now + 1e-9]
        if not able:
            now = min(e[0] for e in todo)
            continue
        e = min(able, key=lambda e: (e[1], e[0]))
        todo.remove(e)
        order.append(e[3])
        now += e[2]
        if e[3][0] == "piece":
            j = e[3][1]
            left[j] -= 1
            if left[j] == 0:
                order.append(("reduce", j))
                if sum(left.values()):
                    todo.append((now + 4.0, 1, 0.2, ("swap", j)))
                else:
                    order += [e[3] for e in todo] + [("swap", j)]
                    todo = []
    return order + [("write", j) for j in range(C)]


def kernel(*refs):
    refs = list(refs)
    take = lambda n: [refs.pop(0) for _ in range(n)]
    stream, hidden, gain, head_in, rewards, kl_terms, resets = take(7)
    values_out, returns_out, head_out, down_out = take(4)
    (X,) = take(1)
    S, ACC, P1, T2, P2, O = take(C), take(C), take(C), take(C), take(C), take(C)
    H, ST, PA, PB, CO, AC, BC, GP, GQ, V, G, HV = take(12)
    ring_send, ring_recv, swap_send, swap_recv, down_send, down_recv, small_send, small_recv, hid_send, hid_recv, over_send, over_recv, local = take(13)

    s, t = lax.axis_index("seq"), lax.axis_index("tp")
    y, z, c = s // 8, (s // 2) % 4, s % 2
    zb, zp, q = z % 2, z // 2, s % 8
    h, x = t // 4, t % 4
    oz, oc = z + 1 - 2 * zb, 1 - c
    fz = z + 2 - 4 * zp
    mine = zb * 2 + c

    def seq(y, z, c):
        return (y * 4 + z) * 2 + c

    def up(d):
        return lax.rem(y + 16 + d, NY)

    def remote(src, dst, send, recv, device):
        return pltpu.make_async_remote_copy(
            src_ref=src, dst_ref=dst, send_sem=send, recv_sem=recv, device_id=device, device_id_type=MESH
        )

    def drain(ref, sem):
        pltpu.make_async_copy(ref, ref, sem).wait()

    line = []
    for d in range(1, 8):
        other = lax.rem(q + d, 8)
        line.append((y * 8 + other, t))
    column = [(seq(up(d), z, c), t) for d in range(1, NY)]
    far = [(seq(up(d), fz, c), t) for d in range(NY)]
    rank = [(s, lax.rem(t + d, NT)) for d in range(1, NT)]
    barrier = pltpu.get_barrier_semaphore()
    peers = line + column + far[1:] + rank
    for peer in peers:
        pl.semaphore_signal(barrier, inc=1, device_id=peer, device_id_type=MESH)

    x_copy = pltpu.make_async_copy(stream, X, local.at[0])
    x_copy.start()
    whole = pltpu.make_async_copy(hidden, HV, local.at[5 + 2 * C])
    whole.start()
    own_copies = []
    for j in range(C):
        own_copies.append(
            pltpu.make_async_copy(stream.at[:, pl.ds(OFFS[j], WIDTHS[j])], S[j].at[y, zp], local.at[1 + j])
        )
        own_copies[-1].start()

    def tokens(yy, zz, cc):
        return pl.ds(pl.multiple_of(seq(yy, zz, cc) * TOK, TOK), TOK)

    row_id = lax.broadcasted_iota(jnp.int32, (TOK, TOK), 0)
    col_id = lax.broadcasted_iota(jnp.int32, (TOK, TOK), 1)

    def to_col(row):
        return jnp.sum(jnp.where(row_id == col_id, row, 0.0), axis=1, keepdims=True)

    def to_row(col):
        return jnp.sum(jnp.where(row_id == col_id, col, 0.0), axis=0, keepdims=True)

    gain_f = gain[...].astype(jnp.float32)
    head = gain_f * head_in[...].astype(jnp.float32)
    head_rows = [head[n : n + 1, :] for n in range(COLS // TOK)]
    res_row = resets[...].astype(jnp.float32)
    before_col = jnp.sum(jnp.where(col_id < row_id, res_row, 0.0), axis=1, keepdims=True)
    before_row = jnp.sum(jnp.where(row_id < col_id, to_col(res_row), 0.0), axis=0, keepdims=True)
    total = jnp.sum(res_row, axis=1, keepdims=True)
    reward_col = to_col(rewards[...] - 0.2 * kl_terms[...])
    reach = (row_id >= col_id) & (before_col == before_row)
    local_row = jnp.sum(jnp.where(reach, reward_col, 0.0), axis=0, keepdims=True)
    pass_row = jnp.where(before_row == total, 1.0, 0.0)

    def put(ref, index, first, second):
        ref[index] = jnp.zeros((8, TOK), jnp.float32)
        ref[index, 0:1, :] = jnp.broadcast_to(first, (1, TOK))
        ref[index, 1:2, :] = jnp.broadcast_to(second, (1, TOK))

    put(PA, q, local_row[:, 0:1], pass_row[:, 0:1])
    x_copy.wait()
    squares, along = jnp.zeros((TOK, TOK), jnp.float32), jnp.zeros((TOK, TOK), jnp.float32)
    for n in range(COLS // TOK):
        xn = X[:, n * TOK : (n + 1) * TOK].astype(jnp.float32)
        squares += xn * xn
        along += xn * head_rows[n]
    put(
        ST,
        t,
        to_row(jnp.sum(squares, axis=1, keepdims=True)),
        to_row(jnp.sum(along, axis=1, keepdims=True)),
    )
    pl.semaphore_wait(barrier, len(peers))

    sends = []

    def go(copy):
        copy.start()
        sends.append(copy)

    def small(kind, ref, index, to):
        for peer in to:
            remote(ref.at[index], ref.at[index], small_send.at[kind], small_recv.at[kind], peer).start()

    def ring(direction, plane, j, hop):
        step = 1 if direction == 0 else -1
        slot = S[j].at[up(-step * (hop - 1)), zp if plane == 0 else 1 - zp]
        src = stream.at[:, pl.ds(OFFS[j], WIDTHS[j])] if (plane, hop) == (0, 1) else slot
        i = ARRIVALS[direction, plane, j, hop]
        return remote(src, slot, ring_send.at[direction * C + j], ring_recv.at[i], (seq(up(step), z, c), t))

    def swap(j):
        return remote(
            stream.at[:, pl.ds(OFFS[j], WIDTHS[j])], S[j].at[y, zp], swap_send.at[j], swap_recv.at[j], (seq(y, fz, c), t)
        )

    small(1, PA, q, line)
    small(0, ST, t, rank)
    first_sends = [{m[1]: at for at, m in ring_plan(d)[0] if m[0] == 0 and m[2] == 1} for d in (0, 1)]
    for j in range(C):
        for direction in (0, 1):
            if first_sends[direction][j] <= START:
                ring(direction, 0, j, 1).start()

    def pair_hidden(i, p, cc):
        yy = 2 * x + i
        return remote(
            HV.at[:, tokens(yy, 1 - zb + 2 * p, cc)], H.at[mine, yy, p],
            hid_send.at[1 + 2 * i + p], hid_recv.at[1 + 2 * i + p], (seq(y, oz, cc), t),
        )

    def do_pair(k):
        for cc in range(2):
            pair_hidden(k // 2, k % 2, cc).start()

    def do_away(j):
        swap(j).start()

    whole.wait()
    do_pair(0)
    do_pair(1)

    def core_hidden(yy, _):
        for p in range(2):
            remote(
                HV.at[:, tokens(yy, zb + 2 * p, oc)], H.at[mine, yy, p],
                hid_send.at[0], hid_recv.at[0], (seq(y, z, oc), t),
            ).start()
        return 0

    def own_hidden(yy, _):
        for p in range(2):
            pltpu.make_async_copy(HV.at[:, tokens(yy, zb + 2 * p, c)], H.at[mine, yy, p], local.at[1 + C]).start()
        return 0

    def do_local():
        lax.fori_loop(0, NY, core_hidden, 0)
        lax.fori_loop(0, NY, own_hidden, 0)

    def pair_block(k, owner):
        return H.at[pl.ds(2 * (1 - zb), 2), 2 * owner + k // 2, k % 2]

    def x_copy_to(direction, k, hop):
        step = 1 if direction == 0 else -1
        block = pair_block(k, lax.rem(x + 8 - step * (hop - 1), NX))
        n = 5 + (hop - 1) * 8 + direction * 4 + k
        return remote(block, block, hid_send.at[n], hid_recv.at[n], (s, h * 4 + lax.rem(x + 4 + step, NX)))

    seen = set()

    def arrived(direction, plane, j, hop):
        if (direction, plane, j, hop) not in seen:
            seen.add((direction, plane, j, hop))
            step = 1 if direction == 0 else -1
            i = ARRIVALS[direction, plane, j, hop]
            drain(S[j].at[up(-step * hop), zp if plane == 0 else 1 - zp], ring_recv.at[i])

    def own_in(j):
        if ("own", j) not in seen:
            seen.add(("own", j))
            own_copies[j].wait()

    def other_in(j):
        if ("swap", j) not in seen:
            seen.add(("swap", j))
            drain(S[j].at[y, 1 - zp], swap_recv.at[j])

    def do_ring(direction, plane, j, hop):
        if hop == 1 and plane == 1:
            other_in(j)
        elif hop > 1:
            arrived(direction, plane, j, hop - 1)
        ring(direction, plane, j, hop).start()

    def x_arrived(direction, k, hop):
        step = 1 if direction == 0 else -1
        owner = lax.rem(x + 8 - step * hop, NX)
        drain(pair_block(k, owner), hid_recv.at[5 + (hop - 1) * 8 + direction * 4 + k])

    def do_over(j, d):
        arrived(0 if d < 0 or d == 4 else 1, 0, j, abs(d))
        slot = S[j].at[up(d), zp]
        k = ROUND_FIRST.index(j)
        remote(slot, slot, over_send.at[k], over_recv.at[k * NY + d + 3], (seq(y, fz, c), t)).start()

    def over_in(j, d):
        drain(S[j].at[up(d), 1 - zp], over_recv.at[ROUND_FIRST.index(j) * NY + d + 3])

    def do_share(k):
        drain(pair_block(k, x), hid_recv.at[1 + k])
        for direction in (0, 1):
            go(x_copy_to(direction, k, 1))

    def do_pass(k):
        x_arrived(k % 2, k, 1)
        go(x_copy_to(k % 2, k, 2))

    def out_small(i):
        src = (V.at[0:1], V.at[1:2], G)[i]
        return pltpu.make_async_copy(src, (values_out, returns_out, head_out)[i], local.at[2 + 2 * C + i])

    def do_first():
        drain(PA.at[pl.ds(0, 7)], small_recv.at[1])
        value, keep = jnp.zeros((1, TOK), jnp.float32), jnp.ones((1, TOK), jnp.float32)
        for i in reversed(range(8)):
            value = PA[i, 0:1, :] + PA[i, 1:2, :] * value
            keep = PA[i, 1:2, :] * keep
        put(PB, y, value, keep)
        small(2, PB, y, column)

    def do_second():
        drain(PB.at[pl.ds(0, 7)], small_recv.at[2])
        carry = jnp.zeros((1, TOK), jnp.float32)
        my_y, my_q = jnp.full((1, TOK), y, jnp.int32), jnp.full((1, TOK), q, jnp.int32)
        for i in reversed(range(NY)):
            carry = jnp.where(my_y < i, PB[i, 0:1, :] + PB[i, 1:2, :] * carry, carry)
        for i in reversed(range(8)):
            carry = jnp.where(my_q < i, PA[i, 0:1, :] + PA[i, 1:2, :] * carry, carry)
        returns = local_row + pass_row * carry
        V[1:2, :] = returns
        out_small(1).start()
        drain(ST.at[pl.ds(0, 7)], small_recv.at[0])
        squares, along = jnp.zeros((1, TOK), jnp.float32), jnp.zeros((1, TOK), jnp.float32)
        for i in range(NT):
            squares += ST[i, 0:1, :]
            along += ST[i, 1:2, :]
        mean = squares * (1.0 / D) + EPS
        scale = lax.rsqrt(mean)
        scale = scale * (1.5 - 0.5 * mean * scale * scale)
        values = scale * along
        V[0:1, :] = values
        out_small(0).start()
        error = values - returns
        put(CO, y * 2 + zp, error * scale, error * (scale * scale * scale * along * (1.0 / D)))
        small(3, CO, y * 2 + zp, column + far)

    def do_coef(i):
        if i == 0:
            drain(CO.at[pl.ds(0, 15)], small_recv.at[3])
        for p in range(2):
            AC[i * 2 + p] = jnp.broadcast_to(to_col(CO[i * 2 + p, 0:1, :]), (TOK, TOK))
            BC[i * 2 + p] = jnp.broadcast_to(to_col(CO[i * 2 + p, 1:2, :]), (TOK, TOK))

    def hidden_in(part):
        if ("hidden", "A") not in seen:
            seen.add(("hidden", "A"))
            drain(H.at[mine], local.at[1 + C])
            drain(H.at[zb * 2 + oc], hid_recv.at[0])
        for name in "BC":
            if name <= part and ("hidden", name) not in seen:
                seen.add(("hidden", name))
                if name == "B":
                    for k in range(4):
                        x_arrived(1 - k % 2, k, 1)
                else:
                    for k in range(4):
                        x_arrived(k % 2, k, 2)

    def block_in(j, plane, d):
        side = 0 if d < 0 or (d == 4 and plane == 0) else 1
        if plane == 1 and d in FAR.get(j, ()):
            over_in(j, d)
        elif d == 0:
            (own_in, other_in)[plane](j)
        else:
            arrived(side, plane, j, abs(d))

    def do_piece(j, plane, group):
        w, off = WIDTHS[j], OFFS[j]
        p = zp if plane == 0 else 1 - zp
        if plane == 0:
            for d in range(-3, 5):
                block_in(j, 0, d)
            hidden_in(group)
            where = [2 * lax.rem(x + 4 + k, NX) + i for k in QUARTERS[group] for i in range(2)]
        else:
            for d in group:
                block_in(j, 1, d)
            hidden_in("C")
            where = [up(d) for d in group]
        grads, rows = [], [[] for _ in range(4)]
        for yy in where:
            a, b = AC[yy * 2 + p], BC[yy * 2 + p]
            xs = S[j][yy, p]
            parts = []
            for i in range(w // TOK):
                xi = xs[:, i * TOK : (i + 1) * TOK].astype(jnp.float32)
                n = off // TOK + i
                GP[yy * 2 + p, n : n + 1, :] = jnp.sum(a * xi, axis=0, keepdims=True)
                parts.append((a * head_rows[n] - b * xi).astype(jnp.bfloat16))
            grads.append(jnp.concatenate(parts, axis=1))
            for r in range(4):
                rows[r].append(H[r, yy, p])
        left = jnp.concatenate([jnp.concatenate(parts, axis=1) for parts in rows], axis=0)
        out = jnp.dot(left, jnp.concatenate(grads, axis=0), preferred_element_type=jnp.float32).reshape(4, ROWS, w)
        if ("sum", j) not in seen:
            seen.add(("sum", j))
            ACC[j][...] = out
        else:
            ACC[j][...] += out

    def core_copy(j, k):
        return remote(
            ACC[j].at[k * 2 + oc], P1[j].at[k], down_send.at[j * 3 + k], down_recv.at[j * 3 + k], (seq(y, z, oc), t)
        )

    def pair_copy(j):
        return remote(T2[j], P2[j], down_send.at[j * 3 + 2], down_recv.at[j * 3 + 2], (seq(y, oz, c), t))

    def do_reduce(j):
        go(core_copy(j, 1 - zb))
        go(core_copy(j, zb))

    def do_swap(j):
        core_copy(j, 1 - zb).wait_recv()
        T2[j][...] = (ACC[j][(1 - zb) * 2 + c] + P1[j][1 - zb]).astype(jnp.bfloat16)
        go(pair_copy(j))
        core_copy(j, zb).wait_recv()

    def out_copy(j):
        return pltpu.make_async_copy(O[j], down_out.at[:, pl.ds(OFFS[j], WIDTHS[j])], local.at[2 + C + j])

    def do_write(j):
        pair_copy(j).wait_recv()
        out = ACC[j][mine] + P1[j][zb] + P2[j][...].astype(jnp.float32)
        O[j][...] = out.astype(jnp.bfloat16)
        out_copy(j).start()

    events = {
        "ring": do_ring, "over": do_over, "share": do_share, "pass": do_pass, "first": do_first, "second": do_second,
        "coef": do_coef, "local": do_local, "pair": do_pair, "away": do_away, "piece": do_piece, "reduce": do_reduce, "swap": do_swap,
        "write": do_write,
    }
    order = timeline()
    last = max(i for i, e in enumerate(order) if e[0] == "piece")
    for i, e in enumerate(order):
        events[e[0]](*e[1:])
        if i == last + 1:
            part = GP[0]
            for k in range(1, 2 * NY):
                part += GP[k]
            GQ[mine] = part
            small(4, GQ, mine, [(seq(y, z, oc), t), (seq(y, oz, c), t), (seq(y, oz, oc), t)])
    drain(GQ.at[pl.ds(0, 3)], small_recv.at[4])
    sums = GQ[0] + GQ[1] + GQ[2] + GQ[3]
    G[...] = gain_f * sums
    out_small(2).start()

    for copy in sends:
        copy.wait_send()
    for kind, ref in enumerate((ST, PA, PB)):
        drain(ref.at[pl.ds(0, 7)], small_send.at[kind])
    drain(CO.at[pl.ds(0, 15)], small_send.at[3])
    drain(GQ.at[pl.ds(0, 3)], small_send.at[4])
    for direction in (0, 1):
        for j in range(C):
            n = sum(hops(direction, plane, j) for plane in (0, 1))
            drain(S[j].at[pl.ds(0, n), 0], ring_send.at[direction * C + j])
    for j in range(C):
        drain(S[j].at[0, 0], swap_send.at[j])
    for k, j in enumerate(ROUND_FIRST):
        drain(S[j].at[pl.ds(0, len(FAR[j])), 0], over_send.at[k])
    drain(H.at[mine], hid_send.at[0])
    for k in range(4):
        drain(pair_block(k, 0), hid_send.at[1 + k])
    for j in range(C):
        out_copy(j).wait()
    for i in range(3):
        out_small(i).wait()


def hand_over(*refs):
    for i in range(4):
        refs[4 + i][...] = refs[i][...]


def scratch():
    f32, bf16 = jnp.float32, jnp.bfloat16
    V, S = pltpu.VMEM, pltpu.SemaphoreType.DMA
    out = [V((TOK, COLS), bf16)]
    out += [V((NY, 2, TOK, w), bf16) for w in WIDTHS]
    out += [V((4, ROWS, w), f32) for w in WIDTHS]
    out += [V((2, ROWS, w), f32) for w in WIDTHS]
    out += [V((ROWS, w), bf16) for w in WIDTHS] * 3
    out += [V((4, NY, 2, ROWS, TOK), bf16)]
    out += [V((n, 8, TOK), f32) for n in (8, 8, 8, 16)]
    out += [V((NY * 2, TOK, TOK), f32)] * 2
    out += [V((NY * 2, 8, TOK), f32), V((4, 8, TOK), f32), V((8, TOK), f32), V((8, TOK), f32)]
    out += [V((ROWS, NY * NZ * 2 * TOK), bf16)]
    out += [S((2 * C,)), S((len(ARRIVALS),)), S((C,)), S((C,)), S((3 * C,)), S((3 * C,))]
    k = max(1, len(ROUND_FIRST))
    out += [S((5,)), S((5,)), S((21,)), S((21,)), S((k,)), S((NY * k,)), S((6 + 2 * C,))]
    return out


def body(stream, hidden, final_gain, value_head, rewards, kl_terms, resets):
    vmem, hbm = pl.BlockSpec(memory_space=pltpu.VMEM), pl.BlockSpec(memory_space=pl.ANY)
    f32 = jnp.float32
    shapes = (
        jax.ShapeDtypeStruct((1, TOK), f32),
        jax.ShapeDtypeStruct((1, TOK), f32),
        jax.ShapeDtypeStruct((8, TOK), f32),
        jax.ShapeDtypeStruct((ROWS, COLS), jnp.bfloat16),
    )
    parts = pl.pallas_call(
        kernel,
        out_shape=shapes,
        in_specs=[hbm, hbm] + [vmem] * 5,
        out_specs=(hbm,) * 4,
        scratch_shapes=scratch(),
        compiler_params=pltpu.CompilerParams(
            collective_id=0, has_side_effects=True, vmem_limit_bytes=60 * 1024 * 1024
        ),
    )(
        stream,
        hidden,
        final_gain.reshape(8, TOK),
        value_head.reshape(8, TOK),
        rewards.reshape(1, TOK),
        kl_terms.reshape(1, TOK),
        resets.reshape(1, TOK),
    )
    values, returns, grad_head, grad_down = pl.pallas_call(
        hand_over, out_shape=shapes, in_specs=[vmem] * 4, out_specs=(vmem,) * 4
    )(*parts)
    return (values.reshape(TOK), returns.reshape(TOK), grad_head.reshape(COLS), grad_down)


def solution(mesh):
    placed = (P("seq", "tp"), P("seq", None), P("tp"), P("tp"), P("seq"), P("seq"), P("seq"))
    return jax.shard_map(
        body,
        mesh=mesh,
        in_specs=placed,
        out_specs=(P("seq"), P("seq"), P("tp"), P("seq", "tp")),
        check_vma=False,
    )
```
